32 devices in a mesh: row: 4 (over z), col: 8 (over y, x, core).
Axes of the slice: x: 2, y: 2, z: 4, core: 2. Of those that a mesh axis runs over, the one named last changes fastest.
Arguments:
- trailing: float32 [16384, 16384], P('row', 'col'), may hold values from -51 to 51
- panel_cols: float32 [16384, 128], P(('row', 'col')), as said below
Outputs:
- updated: float32 [16384, 16384], P('row', 'col')
- triangle: float32 [128, 128], replicated
The draws below stay inside these ranges and needn't reach their ends.
Inputs may be any that keep to these rules, and one draw needn't show every extreme that they name: panel_cols has full column rank.
All inputs are finite; a program needn't handle non-finite values.
Results may differ from the reference program's by a relative error of at most 0.00005.
Values sent between devices are 32-bit elements; how exact they have to be, the bound alone decides.
No kernel may reach another device: no remote copies, remote signals or barrier semaphores. Data moves between devices by JAX's collectives and lax.ppermute only.
A program may use at most 128 MiB of HBM per device.

```python
import math
import jax
import jax.numpy as jnp
from jax import lax

M = 16384
NB = 128


def draw_trailing(key, part):
    first = jax.random.fold_in(key, 11)
    noise = jnp.clip(jax.random.normal(first, (M, M), jnp.float32), -4.0, 4.0)
    result = (noise + noise.T) * 0.70710678
    return result


def draw_panel_cols(key, part):
    first = jax.random.fold_in(key, 21)
    second = jax.random.fold_in(key, 22)
    third = jax.random.fold_in(key, 23)
    noise = jnp.clip(jax.random.normal(first, (M, NB), jnp.float32), -4.0, 4.0) / math.sqrt(M)
    rising = 1.0 + 2.0 * jnp.arange(M, dtype=jnp.float32) / (M - 1)
    rough = jax.random.uniform(second, (M,), jnp.float32, 0.5, 1.5)
    noise = noise * (rising * rough)[:, None]
    mixing = jnp.eye(NB, dtype=jnp.float32) + 0.06 + 0.2 / math.sqrt(NB) * jax.random.normal(third, (NB, NB), jnp.float32)
    return jnp.dot(noise, mixing, precision=lax.Precision.HIGHEST, preferred_element_type=jnp.float32)


def setup_inputs(seed: int = 0) -> dict:
    keys = jax.random.split(jax.random.key(seed), 3)
    trailing = draw_trailing(jax.random.fold_in(keys[2], 71), 0)
    panel_cols = draw_panel_cols(jax.random.fold_in(keys[2], 71), 0)
    return {"trailing": trailing, "panel_cols": panel_cols}


def reference(trailing, panel_cols):
    high = lax.Precision.HIGHEST
    gram_sum = jnp.dot(panel_cols.T.astype(jnp.float32), panel_cols.astype(jnp.float32), precision=high, preferred_element_type=jnp.float32)
    factor = jnp.linalg.cholesky(gram_sum)
    basis = lax.linalg.triangular_solve(factor, panel_cols.T, left_side=True, lower=True).T
    image = jnp.dot(trailing.astype(jnp.float32), basis.astype(jnp.float32), precision=high, preferred_element_type=jnp.float32)
    coupling = jnp.dot(basis.T.astype(jnp.float32), image.astype(jnp.float32), precision=high, preferred_element_type=jnp.float32)
    shifts = 2.0 * image - 2.0 * jnp.dot(basis.astype(jnp.float32), coupling.astype(jnp.float32), precision=high, preferred_element_type=jnp.float32)
    left_side = jnp.concatenate([basis, shifts], axis=1)
    right_side = jnp.concatenate([shifts, basis], axis=1)
    updated = trailing - jnp.dot(left_side.astype(jnp.float32), right_side.T.astype(jnp.float32), precision=high, preferred_element_type=jnp.float32)
    return (updated, factor.T)
```

```python
import functools

import jax
import jax.numpy as jnp
from jax import lax
from jax.experimental import pallas as pl
from jax.experimental.pallas import tpu as pltpu
from jax.sharding import PartitionSpec as P


F32 = jnp.float32
BF16 = jnp.bfloat16
HIGHEST = lax.Precision.HIGHEST
VMEM_LIMIT = 56 * 1024 * 1024


def xor_permute(array, axis, size, step):
    return lax.ppermute(array, axis, [(i, i ^ step) for i in range(size)])


def tree_sum(terms):
    while len(terms) > 1:
        terms = [terms[i] + terms[i + 1] for i in range(0, len(terms), 2)]
    return terms[0]


def split(value):
    high = value.astype(BF16)
    low = (value - high.astype(F32)).astype(BF16)
    return high, low


def matmul_high(left, right):
    return jnp.dot(left, right, precision=HIGHEST, preferred_element_type=F32)


def inner_kernel(count, *refs):
    lefts, rights, out = refs[:count], refs[count : 2 * count], refs[2 * count]
    terms = [
        lax.dot_general(
            a[...], b[...], (((0,), (0,)), ((), ())), precision=HIGHEST, preferred_element_type=F32
        )
        for a, b in zip(lefts, rights)
    ]
    out[...] = tree_sum(terms)


def inner(lefts, rights):
    count = len(lefts)
    rows, width = lefts[0].shape
    return pl.pallas_call(
        functools.partial(inner_kernel, count),
        out_shape=jax.ShapeDtypeStruct((width, width), F32),
        in_specs=[pl.BlockSpec(memory_space=pltpu.VMEM)] * (2 * count),
        out_specs=pl.BlockSpec(memory_space=pltpu.VMEM),
        cost_estimate=pl.CostEstimate(
            flops=12 * count * rows * width * width, bytes_accessed=8 * count * rows * width, transcendentals=0
        ),
    )(*lefts, *rights)


def image_kernel(pieces, where, trailing_ref, *refs):
    parts, out_ref, wide = refs[:pieces], refs[pieces], refs[pieces + 1]
    block = parts[0].shape[0]
    width = parts[0].shape[1]

    @pl.when(pl.program_id(0) == 0)
    def _():
        for step, part in enumerate(parts):
            high, low = split(part[...])
            start = pl.multiple_of((where[1] ^ step) * block, block)
            wide[pl.ds(start, block), :width] = high
            wide[pl.ds(start, block), width:] = low

    high, low = split(trailing_ref[...])
    total = jnp.dot(high, wide[...], preferred_element_type=F32)
    total += jnp.dot(low, wide[...], preferred_element_type=F32)
    out_ref[0] = total[:, :width] + total[:, width:]


def image_part(trailing, parts, where, parity):
    pieces = len(parts)
    block, width = parts[0].shape
    rows, cols = trailing.shape
    steps = rows // block // 2
    return pl.pallas_call(
        functools.partial(image_kernel, pieces),
        out_shape=jax.ShapeDtypeStruct((steps, block, width), F32),
        grid_spec=pltpu.PrefetchScalarGridSpec(
            num_scalar_prefetch=1,
            grid=(steps,),
            in_specs=[pl.BlockSpec((block, cols), lambda s, w: (w[0] ^ (2 * s + parity), 0))]
            + [pl.BlockSpec((block, width), lambda s, w: (0, 0))] * pieces,
            out_specs=pl.BlockSpec((1, block, width), lambda s, w: (s, 0, 0)),
            scratch_shapes=[pltpu.VMEM((cols, 2 * width), BF16)],
        ),
        compiler_params=pltpu.CompilerParams(
            dimension_semantics=("arbitrary",), vmem_limit_bytes=VMEM_LIMIT
        ),
        cost_estimate=pl.CostEstimate(
            flops=4 * rows * cols * width, bytes_accessed=2 * rows * cols, transcendentals=0
        ),
    )(where, trailing, *parts)


def update_kernel(blocks, pieces, where, trailing_ref, *refs):
    panel, image = refs[:blocks], refs[blocks : 2 * blocks]
    panel_cols = refs[2 * blocks : 2 * blocks + pieces]
    image_cols = refs[2 * blocks + pieces : 2 * blocks + 2 * pieces]
    inverse_ref, coupling_ref, out_ref, left, right = refs[2 * blocks + 2 * pieces :]
    block, width = panel[0].shape
    both = 2 * width
    step = pl.program_id(0)

    @pl.when(step == 0)
    def _():
        inverse = inverse_ref[...]
        turn = inverse.T
        normal = matmul_high(inverse, turn)
        mixed = matmul_high(coupling_ref[...], turn)
        factors = jnp.concatenate([2.0 * normal, -4.0 * mixed], axis=0)
        for t in range(pieces):
            start = pl.multiple_of((where[1] ^ t) * block, block)
            basis = matmul_high(panel_cols[t][...], inverse)
            first = matmul_high(jnp.concatenate([image_cols[t][...], basis], axis=1), factors)
            second = 2.0 * matmul_high(basis, turn)
            high, low = split(jnp.concatenate([first, second], axis=1))
            right[pl.ds(start, block), :both] = high
            right[pl.ds(start, block), both : 2 * both] = low
            right[pl.ds(start, block), 2 * both :] = high

    for q in range(blocks):

        @pl.when(step == q)
        def _():
            high, low = split(jnp.concatenate([panel[q][...], image[q][...]], axis=1))
            left[:, :both] = high
            left[:, both : 2 * both] = high
            left[:, 2 * both :] = low

    out_ref[...] = trailing_ref[...] - lax.dot_general(
        left[...], right[...], (((1,), (1,)), ((), ())), preferred_element_type=F32
    )


def update(trailing, panel, image, panel_cols, image_cols, inverse, coupling, where):
    blocks, pieces = len(panel), len(panel_cols)
    block, width = panel[0].shape
    rows, cols = trailing.shape
    whole = pl.BlockSpec((block, width), lambda s, w: (0, 0), pipeline_mode=pl.Buffered(1))
    small = pl.BlockSpec((width, width), lambda s, w: (0, 0))
    return pl.pallas_call(
        functools.partial(update_kernel, blocks, pieces),
        out_shape=jax.ShapeDtypeStruct((rows, cols), F32),
        grid_spec=pltpu.PrefetchScalarGridSpec(
            num_scalar_prefetch=1,
            grid=(blocks,),
            in_specs=[pl.BlockSpec((block, cols), lambda s, w: (w[0] ^ s, 0))]
            + [whole] * (2 * blocks + 2 * pieces)
            + [small] * 2,
            out_specs=pl.BlockSpec((block, cols), lambda s, w: (w[0] ^ s, 0)),
            scratch_shapes=[
                pltpu.VMEM((block, 6 * width), BF16),
                pltpu.VMEM((cols, 6 * width), BF16),
            ],
        ),
        compiler_params=pltpu.CompilerParams(
            dimension_semantics=("arbitrary",), vmem_limit_bytes=VMEM_LIMIT
        ),
        cost_estimate=pl.CostEstimate(
            flops=12 * rows * cols * width, bytes_accessed=8 * rows * cols, transcendentals=0
        ),
    )(where, trailing, *panel, *image, *panel_cols, *image_cols, inverse, coupling)


def gather_rows(block, n_col):
    found = {0: block}
    for q in range(2, n_col, 2):
        found[q] = xor_permute(block, "col", n_col, q)
    for q in range(0, n_col, 2):
        found[q + 1] = xor_permute(found[q], "col", n_col, 1)
    return [found[q] for q in range(n_col)]


def gather_cols(block, n_row, n_col, row_index, col_index):
    near = [block] + [xor_permute(block, "row", n_row, q) for q in range(1, n_row)]
    ratio = n_col // n_row
    turn = (col_index % n_row) ^ row_index
    result = []
    for t in range(n_row):
        chosen = near[t]
        for other in range(1, n_row):
            chosen = jnp.where(turn == other, near[t ^ other], chosen)
        pairs = [(u * n_row + i, (i ^ t) * ratio + u) for u in range(ratio) for i in range(n_row)]
        result.append(lax.ppermute(chosen, "col", pairs))
    return result


def sum_rows(square, n_row):
    return tree_sum([square] + [xor_permute(square, "row", n_row, q) for q in range(1, n_row)])


def local(n_row, n_col, trailing, panel_cols):
    row_index = lax.axis_index("row")
    col_index = lax.axis_index("col")
    where = jnp.stack([col_index, col_index * n_row // n_col]).astype(jnp.int32)

    panel_home = gather_cols(panel_cols, n_row, n_col, row_index, col_index)
    panel_row = gather_rows(panel_cols, n_col)

    away = image_part(trailing, panel_home, where, 1)
    arrived = xor_permute(away, "col", n_col, 1)
    stay = image_part(trailing, panel_home, where, 0)

    gram_sum = sum_rows(inner(panel_row, panel_row), n_row)
    factor = jnp.linalg.cholesky(gram_sum)
    inverse = lax.linalg.triangular_solve(
        factor, jnp.eye(factor.shape[0], dtype=F32), left_side=True, lower=True
    ).T

    halves = stay + arrived
    image_own = tree_sum(
        [halves[0]] + [xor_permute(halves[q], "col", n_col, 2 * q) for q in range(1, n_col // 2)]
    )
    image_row = gather_rows(image_own, n_col)
    image_home = gather_cols(image_own, n_row, n_col, row_index, col_index)

    product = sum_rows(inner(panel_row, image_row), n_row)
    coupling = matmul_high(matmul_high(inverse.T, product), inverse)
    coupling = 0.5 * (coupling + coupling.T)
    updated = update(trailing, panel_row, image_row, panel_home, image_home, inverse, coupling, where)
    return (updated, factor.T)


def solution(mesh):
    n_row, n_col = mesh.shape["row"], mesh.shape["col"]
    in_specs = (P("row", "col"), P(("row", "col"), None))
    out_specs = (P("row", "col"), P())
    return jax.shard_map(
        functools.partial(local, n_row, n_col),
        mesh=mesh,
        in_specs=in_specs,
        out_specs=out_specs,
        check_vma=False,
    )
```

```python
import functools

import jax
import jax.numpy as jnp
from jax import lax
from jax.experimental import pallas as pl
from jax.experimental.pallas import tpu as pltpu
from jax.sharding import PartitionSpec as P


F32 = jnp.float32
BF16 = jnp.bfloat16
HIGHEST = lax.Precision.HIGHEST
VMEM_LIMIT = 56 * 1024 * 1024
LANES = 128
IN_VMEM = pl.BlockSpec(memory_space=pltpu.VMEM)
IN_SMEM = pl.BlockSpec(memory_space=pltpu.SMEM)
COL, HOME, ROW = 0, 1, 2


def permute(array, axis, size, step):
    return lax.ppermute(array, axis, [(i, i ^ step) for i in range(size)])


def after(value, *others):
    return lax.optimization_barrier((value, *others))[0]


def choose(key, arrays):
    chosen = arrays[0]
    for i in range(1, len(arrays)):
        chosen = jnp.where(key == i, arrays[i], chosen)
    return chosen


def tree_sum(terms):
    while len(terms) > 1:
        paired = [terms[i] + terms[i + 1] for i in range(0, len(terms) - 1, 2)]
        terms = paired + terms[2 * len(paired) :]
    return terms[0]


def split(value):
    high = value.astype(BF16)
    low = (value - high.astype(F32)).astype(BF16)
    return high, low


def matmul_high(left, right):
    return jnp.dot(left, right, precision=HIGHEST, preferred_element_type=F32)


def inner_high(left, right):
    return lax.dot_general(
        left, right, (((0,), (0,)), ((), ())), precision=HIGHEST, preferred_element_type=F32
    )


def aligned(index, size):
    return pl.ds(pl.multiple_of(index * size, size), size)


def estimate(flops, read):
    return pl.CostEstimate(flops=int(flops), bytes_accessed=int(read), transcendentals=0)


def gram_kernel(*refs):
    *blocks, out = refs
    out[...] = tree_sum([inner_high(block[...], block[...]) for block in blocks])


def gram(blocks):
    rows, width = blocks[0].shape
    return pl.pallas_call(
        gram_kernel,
        out_shape=jax.ShapeDtypeStruct((width, width), F32),
        in_specs=[IN_VMEM] * len(blocks),
        out_specs=IN_VMEM,
        cost_estimate=estimate(12 * len(blocks) * rows * width**2, 4 * len(blocks) * rows * width),
    )(*blocks)


def image_kernel(count, where, trailing_ref, *refs):
    if count:
        panel, (pair_refs, wide, total) = refs[:count], (refs[count:-2], refs[-2], refs[-1])
    else:
        wide, pair_refs, total = refs[0], refs[1:-1], refs[-1]
    step = pl.program_id(0)
    width = total.shape[0]

    if count:

        @pl.when(step == 0)
        def _():
            for q in range(count):
                high, low = split(panel[q][...].T)
                wide[q, :width] = high
                wide[q, width:] = low

    high, low = split(trailing_ref[...])
    turned = wide[step]
    both = jnp.dot(turned, high, preferred_element_type=F32)
    part = both[:width] + both[width:]
    part += jnp.dot(turned[:width], low, preferred_element_type=F32)

    @pl.when(step == 0)
    def _():
        total[...] = part

    @pl.when(step > 0)
    def _():
        total[...] += part

    @pl.when(step == pl.num_programs(0) - 1)
    def _():
        if len(pair_refs) == 1:
            pair_refs[0][...] = total[...]
        else:
            chunk = pair_refs[0].shape[1]
            place = where[ROW] % 2
            pair_refs[0][...] = total[:, aligned(place, chunk)]
            pair_refs[1][...] = total[:, aligned(1 - place, chunk)]


def image_pair(trailing, panel, wide, where, n_row, n_col, pair):
    rows, cols = trailing.shape
    block, chunk = rows // n_col, cols // n_row
    width = panel[0].shape[1]
    whole = chunk % LANES != 0
    outs = [jax.ShapeDtypeStruct((width, 2 * chunk), F32)] if whole else [jax.ShapeDtypeStruct((width, chunk), F32)] * 2
    out_specs = [pl.BlockSpec(out.shape, lambda s, w: (0, 0)) for out in outs]
    in_specs = [pl.BlockSpec((block, 2 * chunk), lambda s, w: (w[COL] ^ s, (w[ROW] // 2) ^ pair))]
    wide_shape = (n_col, 2 * width, block)
    wide_spec = pl.BlockSpec(wide_shape, lambda s, w: (0, 0, 0), pipeline_mode=pl.Buffered(1))
    if wide is None:
        operands = panel
        in_specs += [pl.BlockSpec(panel[0].shape, lambda s, w: (0, 0), pipeline_mode=pl.Buffered(1))] * n_col
        outs.append(jax.ShapeDtypeStruct(wide_shape, BF16))
        out_specs.append(wide_spec)
    else:
        operands = [wide]
        in_specs.append(wide_spec)
    result = pl.pallas_call(
        functools.partial(image_kernel, n_col if wide is None else 0),
        out_shape=outs,
        grid_spec=pltpu.PrefetchScalarGridSpec(
            num_scalar_prefetch=1,
            grid=(n_col,),
            in_specs=in_specs,
            out_specs=out_specs,
            scratch_shapes=[pltpu.VMEM((width, 2 * chunk), F32)],
        ),
        compiler_params=pltpu.CompilerParams(
            dimension_semantics=("arbitrary",), vmem_limit_bytes=VMEM_LIMIT
        ),
        cost_estimate=estimate(8 * rows * 2 * chunk * width, 4 * rows * 2 * chunk),
    )(where, trailing, *operands)
    if wide is None:
        *result, wide = result
    if whole:
        halves = [result[0][:, :chunk], result[0][:, chunk:]]
        place = where[ROW] % 2
        result = [choose(place, halves), choose(1 - place, halves)]
    return result[0], result[1], wide


def finish_kernel(count, where, *refs):
    terms, own_ref, pieces = refs[:count], refs[count], refs[count + 1 :]
    own_ref[...] = tree_sum([term[...] for term in terms]).T
    size = pieces[0].shape[0]
    for p, piece in enumerate(pieces):
        piece[...] = own_ref[aligned((where[COL] // 2) ^ p, size), :]


def finish(terms, where, chips):
    width, rows = terms[0].shape
    return pl.pallas_call(
        functools.partial(finish_kernel, len(terms)),
        out_shape=[jax.ShapeDtypeStruct((rows, width), F32)]
        + [jax.ShapeDtypeStruct((rows // chips, width), F32)] * chips,
        in_specs=[IN_SMEM] + [IN_VMEM] * len(terms),
        out_specs=[IN_VMEM] * (1 + chips),
        cost_estimate=estimate(len(terms) * rows * width, 8 * len(terms) * rows * width),
    )(where, *terms)


def home_kernel(pieces, where, *refs):
    panel, inverse_ref, basis_ref, second_ref = refs[:pieces], *refs[pieces:]
    block = panel[0].shape[0]
    inverse = inverse_ref[...]
    turn = 2.0 * inverse.T
    for t in range(pieces):
        rows = aligned(where[HOME] ^ t, block)
        basis = matmul_high(panel[t][...], inverse)
        basis_ref[rows, :] = basis
        second_ref[rows, :] = matmul_high(basis, turn)


def home(panel, inverse, where):
    pieces = len(panel)
    block, width = panel[0].shape
    shape = jax.ShapeDtypeStruct((pieces * block, width), F32)
    return pl.pallas_call(
        functools.partial(home_kernel, pieces),
        out_shape=[shape, shape],
        in_specs=[IN_SMEM] + [IN_VMEM] * (pieces + 1),
        out_specs=[IN_VMEM] * 2,
        cost_estimate=estimate(24 * pieces * block * width**2, 12 * pieces * block * width),
    )(where, *panel, inverse)


def product_kernel(pieces, where, basis_ref, *refs):
    image, out = refs[:pieces], refs[pieces]
    block = image[0].shape[0]
    out[...] = tree_sum(
        [inner_high(basis_ref[aligned(where[ROW] ^ q, block), :], image[q][...]) for q in range(pieces)]
    )


def product(basis, image, where):
    pieces = len(image)
    block, width = image[0].shape
    return pl.pallas_call(
        functools.partial(product_kernel, pieces),
        out_shape=jax.ShapeDtypeStruct((width, width), F32),
        in_specs=[IN_SMEM] + [IN_VMEM] * (pieces + 1),
        out_specs=IN_VMEM,
        cost_estimate=estimate(12 * pieces * block * width**2, 8 * pieces * block * width),
    )(where, basis, *image)


def update_kernel(n_row, n_col, scattered, where, trailing_ref, *refs):
    chips = n_col // 2
    panel, refs = refs[:n_col], refs[n_col:]
    image_home, refs = refs[:n_row], refs[n_row:]
    basis_ref, second_ref, inverse_ref, product_ref, *refs = refs
    image_row, (out_ref, left, right) = refs[:-3], refs[-3:]
    block, width = panel[0].shape
    both = 2 * width
    step = pl.program_id(0)

    @pl.when(step == 0)
    def _():
        inverse = inverse_ref[...]
        normal = 2.0 * matmul_high(inverse, inverse.T)
        factors = jnp.concatenate([normal, -2.0 * matmul_high(product_ref[...], normal)], axis=0)
        for q in range(n_row):
            rows = aligned(where[ROW] ^ q, block)
            first = matmul_high(jnp.concatenate([image_home[q][...], basis_ref[rows, :]], axis=1), factors)
            high, low = split(jnp.concatenate([first, second_ref[rows, :]], axis=1))
            right[rows, :both] = high
            right[rows, both : 2 * both] = low
            right[rows, 2 * both :] = high

    def put(rows, start, value):
        high, low = split(value)
        left[rows, start : start + width] = high
        left[rows, both + start : both + start + width] = high
        left[rows, 2 * both + start : 2 * both + start + width] = low

    for q in range(n_col):

        @pl.when(step == q)
        def _():
            put(slice(None), 0, panel[q][...])

    place = where[COL] ^ step
    if scattered:
        group = chips // n_row
        size = block // chips
        parity, chunk, source = place // n_row % 2, place % n_row, place // (2 * n_row)
        for other in range(2):

            @pl.when((parity ^ where[COL]) % 2 == other)
            def _():
                for p in range(chips):
                    chip = (where[COL] // 2) ^ p
                    value = image_row[2 * p + other][chunk ^ where[ROW], source ^ (chip % group)]
                    put(aligned(chip, size), width, value)
    else:
        put(slice(None), width, image_row[0][aligned(place, block), :])

    out_ref[...] = trailing_ref[...] - lax.dot_general(
        left[...], right[...], (((1,), (1,)), ((), ())), preferred_element_type=F32
    )


def update(trailing, panel, image_home, basis, second, inverse, products, image_row, scattered, where):
    n_row, n_col = len(image_home), len(panel)
    block, width = panel[0].shape
    rows, cols = trailing.shape

    def whole(array):
        zeros = (0,) * array.ndim
        return pl.BlockSpec(array.shape, lambda s, w: zeros, pipeline_mode=pl.Buffered(1))

    operands = [*panel, *image_home, basis, second, inverse, products, *image_row]
    return pl.pallas_call(
        functools.partial(update_kernel, n_row, n_col, scattered),
        out_shape=jax.ShapeDtypeStruct((rows, cols), F32),
        grid_spec=pltpu.PrefetchScalarGridSpec(
            num_scalar_prefetch=1,
            grid=(n_col,),
            in_specs=[pl.BlockSpec((block, cols), lambda s, w: (w[COL] ^ s, 0))]
            + [whole(array) for array in operands],
            out_specs=pl.BlockSpec((block, cols), lambda s, w: (w[COL] ^ s, 0)),
            scratch_shapes=[
                pltpu.VMEM((block, 6 * width), BF16),
                pltpu.VMEM((cols, 6 * width), BF16),
            ],
        ),
        compiler_params=pltpu.CompilerParams(
            dimension_semantics=("arbitrary",), vmem_limit_bytes=VMEM_LIMIT
        ),
        cost_estimate=estimate(12 * rows * cols * width, 8 * rows * cols),
    )(where, trailing, *operands)


def gather_panel_row(block, n_col):
    found = {0: block}
    for q in range(2, n_col, 2):
        found[q] = permute(block, "col", n_col, q)
    for q in range(0, n_col, 2):
        found[q + 1] = permute(found[q], "col", n_col, 1)
    return [found[q] for q in range(n_col)]


def gather_along_row(block, n_row):
    found = {0: block, 1: permute(block, "row", n_row, 1)}
    for q in range(2, n_row, 2):
        found[q] = permute(block, "row", n_row, q)
    for q in range(2, n_row, 2):
        found[q + 1] = permute(found[q], "row", n_row, 1)
    return [found[q] for q in range(n_row)]


def gather_panel_home(block, n_row, n_col, row_index, col_index):
    near = gather_along_row(block, n_row)
    ratio = n_col // n_row
    turn = (col_index % n_row) ^ row_index
    result = []
    for t in range(n_row):
        chosen = choose(turn, [near[t ^ other] for other in range(n_row)])
        pairs = [(u * n_row + i, (i ^ t) * ratio + u) for u in range(ratio) for i in range(n_row)]
        result.append(lax.ppermute(chosen, "col", pairs))
    return result


def gather_image_row(pieces, n_row, n_col, row_index, col_index):
    chips = n_col // 2
    group = chips // n_row
    met = [pieces[0]] + [permute(pieces[p], "col", n_col, 2 * p) for p in range(1, chips)]
    turn = (col_index // 2 // group) ^ row_index
    bundles = []
    for r in range(n_row):
        picks = [
            jnp.stack([met[(turn_value ^ r) * group + e] for e in range(group)]) for turn_value in range(n_row)
        ]
        chosen = choose(turn, picks)
        bundles.append(permute(chosen, "row", n_row, r) if r else chosen)
    bundle = jnp.stack(bundles)
    result = []
    for p in range(chips):
        found = permute(bundle, "col", n_col, 2 * p) if p else bundle
        result += [found, permute(found, "col", n_col, 1)]
    return result


def local(n_row, n_col, trailing, panel_cols):
    row_index = lax.axis_index("row")
    col_index = lax.axis_index("col")
    where = jnp.stack([col_index, col_index * n_row // n_col, row_index]).astype(jnp.int32)
    chips = n_col // 2
    chunk = panel_cols.shape[0]
    scattered = chunk % (16 * chips) == 0 and chunk % LANES == 0

    panel_row = gather_panel_row(panel_cols, n_col)
    panel_home = gather_panel_home(panel_cols, n_row, n_col, row_index, col_index)

    wide = None
    kept, sums = {}, []
    for pair in list(range(1, n_row // 2)) + [0]:
        kept[2 * pair], odd, wide = image_pair(trailing, panel_row, wide, where, n_row, n_col, pair)
        if pair:
            kept[2 * pair] += permute(odd, "row", n_row, 1)
        else:
            kept[1] = odd
    terms = [kept[0], permute(kept[1], "row", n_row, 1)]
    terms += [permute(kept[q], "row", n_row, q) for q in range(2, n_row, 2)]

    gram_own = after(gram(panel_row), kept[0])
    gram_sum = tree_sum([gram_own] + [permute(gram_own, "row", n_row, q) for q in range(1, n_row)])
    factor = jnp.linalg.cholesky(gram_sum)
    inverse = lax.linalg.triangular_solve(
        factor, jnp.eye(factor.shape[0], dtype=F32), left_side=True, lower=True
    ).T
    basis, second = home(panel_home, inverse, where)

    if scattered:
        image_own, *pieces = finish(terms, where, chips)
        image_row = gather_image_row(pieces, n_row, n_col, row_index, col_index)
    else:
        image_own = tree_sum(terms).T
        image_all = lax.all_gather(image_own, ("col", "row"), axis=0, tiled=True)
        image_row = [lax.dynamic_slice_in_dim(image_all, row_index * trailing.shape[0], trailing.shape[0], 0)]
    image_home = gather_along_row(image_own, n_row)

    products = product(basis, image_home, where)
    products = products + permute(products, "col", n_col, 1)
    products = tree_sum([products] + [permute(products, "col", n_col, 2 * p) for p in range(1, chips)])
    updated = update(
        trailing, panel_row, image_home, basis, second, inverse, products, image_row, scattered, where
    )
    return (updated, factor.T)


def solution(mesh):
    n_row, n_col = mesh.shape["row"], mesh.shape["col"]
    in_specs = (P("row", "col"), P(("row", "col"), None))
    out_specs = (P("row", "col"), P())
    return jax.shard_map(
        functools.partial(local, n_row, n_col),
        mesh=mesh,
        in_specs=in_specs,
        out_specs=out_specs,
        check_vma=False,
    )
```

```python
import functools

import jax
import jax.numpy as jnp
from jax import lax
from jax.experimental import pallas as pl
from jax.experimental.pallas import tpu as pltpu
from jax.sharding import PartitionSpec as P


F32 = jnp.float32
BF16 = jnp.bfloat16
HIGHEST = lax.Precision.HIGHEST
LANES = 128
SCOPED = 14
IN_VMEM = pl.BlockSpec(memory_space=pltpu.VMEM)
IN_SMEM = pl.BlockSpec(memory_space=pltpu.SMEM)
COL, HOME, ROW = 0, 1, 2


def permute(array, axis, size, step):
    return lax.ppermute(array, axis, [(i, i ^ step) for i in range(size)])


def after(value, *others):
    return lax.optimization_barrier((value, *others))[0]


def tree_sum(terms):
    while len(terms) > 1:
        paired = [terms[i] + terms[i + 1] for i in range(0, len(terms) - 1, 2)]
        terms = paired + terms[2 * len(paired) :]
    return terms[0]


def split(value):
    high = value.astype(BF16)
    low = (value - high.astype(F32)).astype(BF16)
    return high, low


def matmul_high(left, right):
    return jnp.dot(left, right, precision=HIGHEST, preferred_element_type=F32)


def inner_high(left, right):
    return lax.dot_general(
        left, right, (((0,), (0,)), ((), ())), precision=HIGHEST, preferred_element_type=F32
    )


def matmul_three(left, right, contract=(1, 0)):
    dims = (((contract[0],), (contract[1],)), ((), ()))
    left_high, left_low = split(left)
    right_high, right_low = split(right)
    doubled = lax.dot_general(
        jnp.concatenate([left_high, left_low], axis=contract[0]),
        jnp.concatenate([right_high, right_high], axis=contract[1]),
        dims,
        preferred_element_type=F32,
    )
    return doubled + lax.dot_general(left_high, right_low, dims, preferred_element_type=F32)


def aligned(index, size):
    return pl.ds(pl.multiple_of(index * size, size), size)


def estimate(flops, read):
    return pl.CostEstimate(flops=int(flops), bytes_accessed=int(read), transcendentals=0)


def room(**others):
    return pltpu.CompilerParams(vmem_limit_bytes=SCOPED * 1024 * 1024, **others)


def call(kernel, held, where, operands, out_shape, reads=False, **others):
    outs, scratch = len(out_shape), list(others.pop("scratch_shapes", ()))
    inputs = 1 + len(operands)

    def body(where_ref, held_ref, *refs):
        ahead = (where_ref, held_ref) if reads else (where_ref,)
        kernel(*ahead, *refs[: inputs - 1 + outs], *refs[inputs + outs :])

    results = pl.pallas_call(
        body,
        out_shape=[*out_shape, pltpu.VMEM(held.shape, held.dtype)],
        grid_spec=pltpu.PrefetchScalarGridSpec(
            num_scalar_prefetch=1,
            grid=others.pop("grid", (1,)),
            in_specs=[IN_VMEM] * inputs,
            out_specs=[IN_VMEM] * (outs + 1),
            scratch_shapes=scratch,
        ),
        input_output_aliases={1: outs},
        compiler_params=room(dimension_semantics=("arbitrary",)),
        **others,
    )(where, held, *operands)
    *found, held = results
    return found, pltpu.with_memory_space_constraint(held, pltpu.VMEM)


def load_kernel(parts, source, target, sems):
    size = source.shape[0] // parts
    copies = [
        pltpu.make_async_copy(
            source.at[pl.ds(i * size, size)], target.at[pl.ds(i * size, size)], sems.at[i]
        )
        for i in range(parts)
    ]
    for copy in copies:
        copy.start()
    for copy in copies:
        copy.wait()


def load(array):
    parts = 8
    kept = pl.pallas_call(
        functools.partial(load_kernel, parts),
        out_shape=pltpu.VMEM(array.shape, array.dtype),
        in_specs=[pl.BlockSpec(memory_space=pl.ANY)],
        out_specs=IN_VMEM,
        scratch_shapes=[pltpu.SemaphoreType.DMA((parts,))],
        compiler_params=room(),
        cost_estimate=estimate(0, 8 * array.size),
    )(array)
    return pltpu.with_memory_space_constraint(kept, pltpu.VMEM)


def gram_kernel(block_ref, out_ref):
    block = block_ref[...]
    out_ref[...] = inner_high(block, block)


def gram(block):
    rows, width = block.shape
    return pl.pallas_call(
        gram_kernel,
        out_shape=jax.ShapeDtypeStruct((width, width), F32),
        in_specs=[IN_VMEM],
        out_specs=IN_VMEM,
        compiler_params=room(),
        cost_estimate=estimate(12 * rows * width**2, 4 * rows * width),
    )(block)


def factor_kernel(where, gram_ref, triangle_ref, inverse_ref, work, turned):
    width = gram_ref.shape[0]
    tall = 8
    work[...] = gram_ref[...]
    row = lax.broadcasted_iota(jnp.int32, (width, width), 0)
    lane = lax.broadcasted_iota(jnp.int32, (width, width), 1)
    turned[...] = (row == lane).astype(F32)
    place = lax.broadcasted_iota(jnp.int32, (tall, width), 0)
    column = lax.broadcasted_iota(jnp.int32, (tall, width), 1)
    for start in range(0, width, tall):
        rows = pl.ds(start, tall)
        upper, other = work[rows, :], turned[rows, :]
        for j in range(tall):
            pivot = upper[j : j + 1, start + j : start + j + 1]
            scale = lax.rsqrt(pivot)
            scale = scale * (1.5 - 0.5 * pivot * scale * scale)
            below = jnp.where(place > j, upper[:, start + j : start + j + 1], 0.0) * (scale * scale)
            line, mirror = upper[j : j + 1, :], other[j : j + 1, :]
            upper = jnp.where(place == j, line * scale, upper - below * line)
            other = jnp.where(place == j, mirror * scale, other - below * mirror)
        triangle_ref[rows, :] = jnp.where(column >= place + start, upper, 0.0)
        turned[rows, :] = other
        if start + tall < width:
            later = jnp.where(column >= start + tall, upper, 0.0)
            work[...] -= inner_high(later, later)
            turned[...] -= inner_high(later, other)
    inverse_ref[...] = turned[...].T


def factorize(gram_sum, held, where):
    shape = jax.ShapeDtypeStruct(gram_sum.shape, F32)
    return call(
        factor_kernel,
        held,
        where,
        [gram_sum],
        [shape, shape],
        scratch_shapes=[pltpu.VMEM(gram_sum.shape, F32)] * 2,
        cost_estimate=estimate(4_000_000_000, 8 * gram_sum.size),
    )


def pick_kernel(count, group, key_of, where, *refs):
    arrays, outs = refs[: count * group], refs[count * group :]
    key = key_of(where)
    for value in range(count):

        @pl.when(key == value)
        def _():
            for r, out in enumerate(outs):
                for e in range(group):
                    out[e] = arrays[(value ^ r) * group + e][...]


def pick(arrays, key_of, count, held, where):
    group = len(arrays) // count
    return call(
        functools.partial(pick_kernel, count, group, key_of),
        held,
        where,
        arrays,
        [jax.ShapeDtypeStruct((group, *arrays[0].shape), F32)] * count,
        cost_estimate=estimate(0, 8 * len(arrays) * arrays[0].size),
    )


def image_kernel(count, pair, where, trailing_ref, *refs):
    if count:
        panel, (pair_refs, wide, total) = refs[:count], (refs[count:-2], refs[-2], refs[-1])
    else:
        wide, pair_refs, total = refs[0], refs[1:-1], refs[-1]
    step = pl.program_id(0)
    width = total.shape[0]

    if count:

        @pl.when(step == 0)
        def _():
            for q in range(count):
                high, low = split(panel[q][...].T)
                wide[q, :width] = high
                wide[q, width:] = low

    rows = aligned(where[COL] ^ step, wide.shape[2])
    high, low = split(trailing_ref[rows, aligned((where[ROW] // 2) ^ pair, total.shape[1])])
    turned = wide[step]
    both = jnp.dot(turned, high, preferred_element_type=F32)
    part = both[:width] + both[width:]
    part += jnp.dot(turned[:width], low, preferred_element_type=F32)

    @pl.when(step == 0)
    def _():
        total[...] = part

    @pl.when(step > 0)
    def _():
        total[...] += part

    @pl.when(step == pl.num_programs(0) - 1)
    def _():
        if len(pair_refs) == 1:
            pair_refs[0][...] = total[...]
        else:
            chunk = pair_refs[0].shape[1]
            place = where[ROW] % 2
            pair_refs[0][...] = total[:, aligned(place, chunk)]
            pair_refs[1][...] = total[:, aligned(1 - place, chunk)]


def image_pair(held, panel, wide, where, n_row, n_col, pair):
    rows, cols = held.shape
    block, chunk = rows // n_col, cols // n_row
    width = panel[0].shape[1]
    whole = chunk % LANES != 0
    outs = [(width, 2 * chunk)] if whole else [(width, chunk)] * 2
    outs = [jax.ShapeDtypeStruct(shape, F32) for shape in outs]
    if wide is None:
        outs.append(jax.ShapeDtypeStruct((n_col, 2 * width, block), BF16))
    result, held = call(
        functools.partial(image_kernel, n_col if wide is None else 0, pair),
        held,
        where,
        panel if wide is None else [wide],
        outs,
        reads=True,
        grid=(n_col,),
        scratch_shapes=[pltpu.VMEM((width, 2 * chunk), F32)],
        cost_estimate=estimate(16 * rows * 2 * chunk * width, 4 * rows * width),
    )
    if wide is None:
        *result, wide = result
    if whole:
        halves = [result[0][:, :chunk], result[0][:, chunk:]]
        result, held = pick(halves, lambda w: w[ROW] % 2, 2, held, where)
        result = [half[0] for half in result]
    return result[0], result[1], wide, held


def finish_kernel(count, where, *refs):
    terms, own_ref, pieces = refs[:count], refs[count], refs[count + 1 :]
    own_ref[...] = tree_sum([term[...] for term in terms]).T
    size = pieces[0].shape[0]
    for p, piece in enumerate(pieces):
        piece[...] = own_ref[aligned((where[COL] // 2) ^ p, size), :]


def finish(terms, chips, held, where):
    width, rows = terms[0].shape
    shapes = [(rows, width)] + [(rows // chips, width)] * chips
    return call(
        functools.partial(finish_kernel, len(terms)),
        held,
        where,
        terms,
        [jax.ShapeDtypeStruct(shape, F32) for shape in shapes],
        cost_estimate=estimate(len(terms) * rows * width, 8 * len(terms) * rows * width),
    )


def home_kernel(pieces, where, *refs):
    panel, inverse_ref, basis_ref, second_ref = refs[:pieces], *refs[pieces:]
    block = panel[0].shape[0]
    inverse = inverse_ref[...]
    turn = 2.0 * inverse.T
    for t in range(pieces):
        rows = aligned(where[HOME] ^ t, block)
        basis = matmul_high(panel[t][...], inverse)
        basis_ref[rows, :] = basis
        second_ref[rows, :] = matmul_three(basis, turn)


def home(panel, inverse, held, where):
    pieces = len(panel)
    block, width = panel[0].shape
    shape = jax.ShapeDtypeStruct((pieces * block, width), F32)
    return call(
        functools.partial(home_kernel, pieces),
        held,
        where,
        [*panel, inverse],
        [shape, shape],
        cost_estimate=estimate(24 * pieces * block * width**2, 12 * pieces * block * width),
    )


def product_kernel(pieces, where, basis_ref, *refs):
    image, out = refs[:pieces], refs[pieces]
    block = image[0].shape[0]
    out[...] = tree_sum(
        [
            matmul_three(basis_ref[aligned(where[ROW] ^ q, block), :], image[q][...], (0, 0))
            for q in range(pieces)
        ]
    )


def product(basis, image, held, where):
    pieces = len(image)
    block, width = image[0].shape
    (result,), held = call(
        functools.partial(product_kernel, pieces),
        held,
        where,
        [basis, *image],
        [jax.ShapeDtypeStruct((width, width), F32)],
        cost_estimate=estimate(12 * pieces * block * width**2, 8 * pieces * block * width),
    )
    return result, held


def update_kernel(n_row, n_col, scattered, where, trailing_ref, *refs):
    chips = n_col // 2
    panel, refs = refs[:n_col], refs[n_col:]
    image_home, refs = refs[:n_row], refs[n_row:]
    basis_ref, second_ref, inverse_ref, product_ref, *refs = refs
    image_row, (out_ref, left, right) = refs[:-3], refs[-3:]
    block, width = panel[0].shape
    both = 2 * width
    step, half = pl.program_id(0), pl.program_id(1)
    part = out_ref.shape[0]

    @pl.when((step == 0) & (half == 0))
    def _():
        inverse = inverse_ref[...]
        normal = 2.0 * matmul_high(inverse, inverse.T)
        factors = jnp.concatenate([normal, -2.0 * matmul_high(product_ref[...], normal)], axis=0)
        for q in range(n_row):
            rows = aligned(where[ROW] ^ q, block)
            first = matmul_three(jnp.concatenate([image_home[q][...], basis_ref[rows, :]], axis=1), factors)
            high, low = split(jnp.concatenate([first, second_ref[rows, :]], axis=1))
            right[rows, :both] = high
            right[rows, both : 2 * both] = low
            right[rows, 2 * both :] = high

    def put(rows, start, value):
        high, low = split(value)
        left[rows, start : start + width] = high
        left[rows, both + start : both + start + width] = high
        left[rows, 2 * both + start : 2 * both + start + width] = low

    for q in range(n_col):

        @pl.when((step == q) & (half == 0))
        def _():
            put(slice(None), 0, panel[q][...])

    place = where[COL] ^ step
    if scattered:
        group = chips // n_row
        size = block // chips
        parity, chunk, source = place // n_row % 2, place % n_row, place // (2 * n_row)
        for other in range(2):

            @pl.when(((parity ^ where[COL]) % 2 == other) & (half == 0))
            def _():
                for p in range(chips):
                    chip = (where[COL] // 2) ^ p
                    value = image_row[2 * p + other][chunk ^ where[ROW], source ^ (chip % group)]
                    put(aligned(chip, size), width, value)
    else:

        @pl.when(half == 0)
        def _():
            put(slice(None), width, image_row[0][aligned(place, block), :])

    out_ref[...] = trailing_ref[aligned(2 * place + half, part), :] - lax.dot_general(
        left[aligned(half, part), :], right[...], (((1,), (1,)), ((), ())), preferred_element_type=F32
    )


def update(trailing, panel, image_home, basis, second, inverse, products, image_row, scattered, where):
    n_row, n_col = len(image_home), len(panel)
    block, width = panel[0].shape
    rows, cols = trailing.shape

    operands = [*panel, *image_home, basis, second, inverse, products, *image_row]
    return pl.pallas_call(
        functools.partial(update_kernel, n_row, n_col, scattered),
        out_shape=jax.ShapeDtypeStruct((rows, cols), F32),
        grid_spec=pltpu.PrefetchScalarGridSpec(
            num_scalar_prefetch=1,
            grid=(n_col, 2),
            in_specs=[IN_VMEM] * (1 + len(operands)),
            out_specs=pl.BlockSpec((block // 2, cols), lambda s, h, w: (2 * (w[COL] ^ s) + h, 0)),
            scratch_shapes=[
                pltpu.VMEM((block, 6 * width), BF16),
                pltpu.VMEM((cols, 6 * width), BF16),
            ],
        ),
        compiler_params=room(dimension_semantics=("arbitrary", "arbitrary")),
        cost_estimate=estimate(12 * rows * cols * width, 8 * rows * cols),
    )(where, trailing, *operands)


def gather_panel_row(block, n_col):
    found = {0: block}
    for q in range(2, n_col, 2):
        found[q] = permute(block, "col", n_col, q)
    for q in range(0, n_col, 2):
        found[q + 1] = permute(found[q], "col", n_col, 1)
    return [found[q] for q in range(n_col)]


def gather_along_row(block, n_row):
    found = {0: block, 1: permute(block, "row", n_row, 1)}
    for q in range(2, n_row, 2):
        found[q] = permute(block, "row", n_row, q)
    for q in range(2, n_row, 2):
        found[q + 1] = permute(found[q], "row", n_row, 1)
    return [found[q] for q in range(n_row)]


def gather_panel_home(near, n_row, n_col, held, where):
    ratio = n_col // n_row
    turned, held = pick(near, lambda w: (w[COL] % n_row) ^ w[ROW], n_row, held, where)
    result = []
    for t in range(n_row):
        pairs = [(u * n_row + i, (i ^ t) * ratio + u) for u in range(ratio) for i in range(n_row)]
        result.append(lax.ppermute(turned[t][0], "col", pairs))
    return result, held


def gather_image_row(pieces, n_row, n_col, held, where):
    chips = n_col // 2
    group = chips // n_row
    met = [pieces[0]] + [permute(pieces[p], "col", n_col, 2 * p) for p in range(1, chips)]
    turned, held = pick(met, lambda w: (w[COL] // 2 // group) ^ w[ROW], n_row, held, where)
    bundles = [turned[0]] + [permute(turned[r], "row", n_row, r) for r in range(1, n_row)]
    bundle = jnp.stack(bundles)
    result = []
    for p in range(chips):
        found = permute(bundle, "col", n_col, 2 * p) if p else bundle
        result += [found, permute(found, "col", n_col, 1)]
    return result, held


def local(n_row, n_col, trailing, panel_cols):
    row_index = lax.axis_index("row")
    col_index = lax.axis_index("col")
    where = jnp.stack([col_index, col_index * n_row // n_col, row_index]).astype(jnp.int32)
    chips = n_col // 2
    chunk = panel_cols.shape[0]
    scattered = chunk % (16 * chips) == 0 and chunk % LANES == 0

    panel_row = gather_panel_row(panel_cols, n_col)
    panel_near = gather_along_row(panel_cols, n_row)
    gram_sum = gram(panel_cols)
    gram_sum += permute(gram_sum, "col", n_col, 1)
    trailing, where, gram_sum = lax.optimization_barrier((trailing, where, gram_sum))
    gram_sum = tree_sum([gram_sum] + [permute(gram_sum, "col", n_col, q) for q in range(2, n_col, 2)])
    held = load(trailing)
    gram_sum = tree_sum([gram_sum] + [permute(gram_sum, "row", n_row, q) for q in range(1, n_row)])

    wide = None
    kept = {}
    for pair in list(range(1, n_row // 2)) + [0]:
        kept[2 * pair], odd, wide, held = image_pair(held, panel_row, wide, where, n_row, n_col, pair)
        if pair:
            kept[2 * pair] += permute(odd, "row", n_row, 1)
        else:
            kept[1] = odd
    terms = [kept[0], permute(kept[1], "row", n_row, 1)]
    terms += [permute(kept[q], "row", n_row, q) for q in range(2, n_row, 2)]

    panel_home, held = gather_panel_home(panel_near, n_row, n_col, held, where)
    (triangle, inverse), held = factorize(gram_sum, held, where)

    if scattered:
        (image_own, *pieces), held = finish(terms, chips, held, where)
        image_row, held = gather_image_row(pieces, n_row, n_col, held, where)
    else:
        image_own = tree_sum(terms).T
        image_all = lax.all_gather(image_own, ("col", "row"), axis=0, tiled=True)
        image_row = [lax.dynamic_slice_in_dim(image_all, row_index * trailing.shape[0], trailing.shape[0], 0)]
    image_home = gather_along_row(image_own, n_row)

    (basis, second), held = home(panel_home, inverse, held, where)
    products, held = product(basis, image_home, held, where)
    products = products + permute(products, "col", n_col, 1)
    products = tree_sum([products] + [permute(products, "col", n_col, 2 * p) for p in range(1, chips)])
    updated = update(
        held, panel_row, image_home, basis, second, inverse, products, image_row, scattered, where
    )
    return (updated, triangle)


def solution(mesh):
    n_row, n_col = mesh.shape["row"], mesh.shape["col"]
    in_specs = (P("row", "col"), P(("row", "col"), None))
    out_specs = (P("row", "col"), P())
    return jax.shard_map(
        functools.partial(local, n_row, n_col),
        mesh=mesh,
        in_specs=in_specs,
        out_specs=out_specs,
        check_vma=False,
    )
```
